256 devices in a mesh: rx: 16 (over x, z_lo), ry: 16 (over z_hi, y, core).
Axes of the slice: x: 4, y: 4, z: 8 (z_hi: 2, z_lo: 4; z = z_hi * 4 + z_lo), core: 2. Of those that a mesh axis runs over, the one named last changes fastest.
Arguments:
- clean: bfloat16 [16, 16, 4, 2, 192, 1024], P('rx', 'ry'), may hold values from -6 to 6
- noise: bfloat16 [16, 16, 4, 2, 192, 1024], P('rx', 'ry'), may hold values from -6 to 6
- noise_level: int32 [16, 16, 4, 2], P('rx', 'ry'), may hold values from 0 to 31
- weight: float32 [16, 16, 9, 192, 192], P('rx', 'ry'), may hold values from -6 to 6
- velocity: float32 [16, 16, 9, 192, 192], P('rx', 'ry'), may hold values from -0.6 to 0.6
Outputs:
- new_weight: float32 [16, 16, 9, 192, 192], P('rx', 'ry')
- new_velocity: float32 [16, 16, 9, 192, 192], P('rx', 'ry')
The draws below stay inside these ranges and needn't reach their ends.
All inputs are finite; a program needn't handle non-finite values.
Results may differ from the reference program's by a relative error of at most 0.0066.
Values sent between devices are 32-bit elements; how exact they have to be, the bound alone decides.
A program may use at most 192 MiB of HBM per device.

```python
import math
import jax
import jax.numpy as jnp
from jax import lax

C = 192
RES = 32
BATCH = 2
STEPS = 4
LEVELS = 32
N_RX = 16
N_RY = 16


def place_ends(entries, rng, smallest, largest):
    extent = entries.shape
    index_at = [jax.random.randint(jax.random.fold_in(rng, axis), (), 0, extent[axis]) for axis in range(len(extent))]
    entries = entries.at[tuple(index_at)].set(smallest)
    longest = extent.index(max(extent))
    index_at[longest] = (index_at[longest] + 1) % extent[longest]
    return entries.at[tuple(index_at)].set(largest)


def shard_levels(key, dims, pieces, least, largest):
    def one(axis_at, shards_of):
        draws = jax.random.uniform(jax.random.fold_in(jax.random.fold_in(key, 6), axis_at), (shards_of,), jnp.float32, least / len(pieces), largest / len(pieces))
        return jnp.repeat(jnp.exp(draws), dims[axis_at] // shards_of).reshape((-1,) + (1,) * (len(dims) - axis_at - 1))

    factor_of = one(*pieces[0])
    for cut in pieces[1:]:
        factor_of = factor_of * one(*cut)
    return factor_of


def scatter_about(key, dims, spread, reach, split=(), kind=jnp.bfloat16):
    loudness = shard_levels(key, dims, split, -0.22, 0.18) if split else 1.0
    drawn = jax.random.normal(key, dims, jnp.float32) * spread * loudness
    return jnp.minimum(jnp.maximum(drawn, -reach), reach).astype(kind)


def setup_inputs(seed: int = 0) -> dict:
    key_list = jax.random.split(jax.random.key(seed), 6)
    return {
        "clean": scatter_about(key_list[0], (N_RX, N_RY, STEPS, BATCH, C, RES * RES), 1.0, 6.0, ((0, 16), (1, 16))),
        "noise": scatter_about(key_list[1], (N_RX, N_RY, STEPS, BATCH, C, RES * RES), 1.0, 6.0, ((0, 16), (1, 16))),
        "noise_level": place_ends(jax.random.randint(key_list[2], (N_RX, N_RY, STEPS, BATCH), 0, LEVELS), jax.random.fold_in(key_list[2], 1), 0, LEVELS - 1).astype(jnp.int32),
        "weight": scatter_about(key_list[3], (N_RX, N_RY, 9, C, C), 1.0, 6.0, ((0, 16), (1, 16)), jnp.float32),
        "velocity": scatter_about(key_list[4], (N_RX, N_RY, 9, C, C), 0.1, 0.6, ((0, 16), (1, 16)), jnp.float32),
    }


norm_epsilon = 1e-05
momentum_decay = 0.9
learn_rate = 50.0
silu_scale = 0.596

def prepare(weight):
    fan = weight.shape[0] * weight.shape[1]
    mean_square = lax.optimization_barrier(jnp.mean(weight * weight, axis=(0, 1)))
    radius = jnp.sqrt(mean_square + norm_epsilon)
    w_eff = (weight / (radius * math.sqrt(fan))).astype(jnp.bfloat16)
    return (w_eff.reshape(fan, weight.shape[2]), radius)

def columns(latents):
    batch_rows, channels, cells = latents.shape
    grid = latents.reshape(batch_rows, channels, RES, RES)
    padded = jnp.pad(grid, ((0, 0), (0, 0), (1, 1), (1, 1)))
    taps = [padded[:, :, row:row + RES, col:col + RES] for row in range(3) for col in range(3)]
    return jnp.stack(taps, axis=1).reshape(batch_rows, 9 * channels, cells)

def input_columns(clean_s, noise_s, level_s):
    sigma = 0.2 * 25.0 ** (level_s.astype(jnp.float32) / (LEVELS - 1))
    c_in = 1.0 / jnp.sqrt(sigma * sigma + 0.25)
    noisy = c_in[:, None, None] * (clean_s.astype(jnp.float32) + sigma[:, None, None] * noise_s.astype(jnp.float32))
    return columns(noisy.astype(jnp.bfloat16))

def out_grad(w_flat, cols, clean_s, norm_count):
    z_value = jnp.einsum('kc,bkp->bcp', w_flat, cols, preferred_element_type=jnp.float32)
    sig = jax.nn.sigmoid(z_value)
    pred = z_value * sig / silu_scale
    error = pred - clean_s.astype(jnp.float32)
    return (2.0 * error * sig * (1.0 + z_value * (1.0 - sig)) / (silu_scale * norm_count)).astype(jnp.bfloat16)

def raw_grad(grad_eff, weight, radius):
    fan = weight.shape[0] * weight.shape[1]
    inner = lax.optimization_barrier(jnp.sum(grad_eff * weight, axis=(0, 1)))
    return (grad_eff / radius - weight * inner / (fan * radius ** 3)) / math.sqrt(fan)

def local_step(weight, velocity, clean_s, noise_s, level_s):
    w_flat, radius = prepare(weight)
    norm_count = clean_s.shape[0] * clean_s.shape[2]
    cols = input_columns(clean_s, noise_s, level_s)
    dz_value = out_grad(w_flat, cols, clean_s, norm_count)
    grad_eff = jnp.einsum('bkp,bcp->kc', cols, dz_value, preferred_element_type=jnp.float32).reshape(weight.shape)
    grad = raw_grad(grad_eff, weight, radius)
    velocity = momentum_decay * velocity + learn_rate * grad
    return (weight - velocity, velocity)

def partner_first(array, distance):
    total = array.shape[0]
    blocks = array.reshape((total // (2 * distance), 2, distance) + array.shape[1:])
    return jnp.flip(blocks, axis=1).reshape(array.shape)

def reference(clean, noise, noise_level, weight, velocity):
    n_first, n_second = (weight.shape[0], weight.shape[1])
    replicas = n_first * n_second
    for step in range(STEPS):

        def per_replica(items):
            return local_step(*items)
        flat = (weight.reshape((replicas,) + weight.shape[2:]), velocity.reshape((replicas,) + velocity.shape[2:]), clean[:, :, step].reshape((replicas,) + clean.shape[3:]), noise[:, :, step].reshape((replicas,) + noise.shape[3:]), noise_level[:, :, step].reshape((replicas,) + noise_level.shape[3:]))
        local, velocity_flat = lax.map(per_replica, flat)
        local = local.reshape(weight.shape)
        velocity = velocity_flat.reshape(velocity.shape)
        if step % 2 == 0:
            distance = n_first // 2 ** (1 + step // 2)
            other = partner_first(local, distance)
        else:
            distance = n_second // 2 ** (1 + step // 2)
            other = jnp.swapaxes(partner_first(jnp.swapaxes(local, 0, 1), distance), 0, 1)
        weight = 0.5 * (local + other)
    return (weight, velocity)
```

```python
import math

import jax
import jax.numpy as jnp
from jax import lax
from jax.experimental import pallas as pl
from jax.experimental.pallas import tpu as pltpu
from jax.sharding import PartitionSpec as P

RES = 32
CELLS = RES * RES
STEPS = 4
LEVELS = 32
C = 192
TAPS = 9
FAN = TAPS * C
OC = 16
HALF = OC // 2
ROWS = OC + HALF
CHUNKS = C // OC
BATCH = 2

norm_epsilon = 1e-05
momentum_decay = 0.9
learn_rate = 50.0
silu_scale = 0.596
MESH = pl.DeviceIdType.MESH
F32 = jnp.float32
BF16 = jnp.bfloat16


def partner_of(step):
    rx, ry = lax.axis_index("rx"), lax.axis_index("ry")
    odd = step % 2
    bit_x = (8 - 2 * step) * (1 - odd)
    bit_y = (10 - 2 * step) * odd
    px = rx + bit_x * (1 - 2 * ((rx // (bit_x + odd)) % 2))
    py = ry + bit_y * (1 - 2 * ((ry // (bit_y + 1 - odd)) % 2))
    return {"rx": px, "ry": py}


def pack(full):
    rest = full[:, :, 128:]
    return full[:, :, :128], jnp.concatenate([rest[:, :HALF], rest[:, HALF:]], axis=-1)


def unpack(packed):
    rest = packed[:, OC:]
    rest = jnp.concatenate([rest[:, :, :64], pltpu.roll(rest, 64, 2)[:, :, :64]], axis=1)
    return jnp.concatenate([packed[:, :OC], rest], axis=-1)


def roll_cells(array, by):
    return pltpu.roll(array, by % CELLS, 1)


def kernel(
    level_ref, clean_hbm, noise_hbm, w_hbm, v_hbm, new_w_hbm, new_v_hbm,
    clean, noise, w_in, v_in, x_ref, xt_ref, mine, other, vel, w_out, v_out,
    in_sem, wv_sem, out_sem, send_sem, recv_sem,
):
    pltpu.make_async_copy(w_hbm.at[0, 0], w_in, wv_sem.at[0]).start()
    pltpu.make_async_copy(v_hbm.at[0, 0], v_in, wv_sem.at[1]).start()
    for step in range(STEPS):
        pltpu.make_async_copy(clean_hbm.at[0, 0, step], clean.at[step], in_sem.at[0, step]).start()
        pltpu.make_async_copy(noise_hbm.at[0, 0, step], noise.at[step], in_sem.at[1, step]).start()

    barrier = pltpu.get_barrier_semaphore()
    for step in range(STEPS):
        pl.semaphore_signal(barrier, inc=1, device_id=partner_of(step), device_id_type=MESH)

    pltpu.make_async_copy(w_hbm.at[0, 0], w_in, wv_sem.at[0]).wait()
    pltpu.make_async_copy(v_hbm.at[0, 0], v_in, wv_sem.at[1]).wait()

    def turn(tap, carry):
        wt = jnp.transpose(w_in[tap])
        rest = wt[:, 128:].reshape(CHUNKS, 2, HALF, 64)
        rest = jnp.concatenate([rest[:, 0], rest[:, 1]], axis=-1)
        for slot in (mine, other):
            slot[0, :, tap, :OC, :] = wt[:, :128].reshape(CHUNKS, OC, 128)
            slot[0, :, tap, OC:, :] = rest
        vel[tap] = jnp.transpose(v_in[tap])
        return carry

    lax.fori_loop(0, TAPS, turn, 0)

    pl.semaphore_wait(barrier, STEPS)

    lane = lax.broadcasted_iota(jnp.int32, (1, CELLS), 1)
    row, col = lane // RES, lane % RES
    ok_row = {-1: row > 0, 1: row < RES - 1}
    ok_col = {-1: col > 0, 1: col < RES - 1}

    def prepare(step):
        pltpu.make_async_copy(clean_hbm.at[0, 0, step], clean.at[step], in_sem.at[0, step]).wait()
        pltpu.make_async_copy(noise_hbm.at[0, 0, step], noise.at[step], in_sem.at[1, step]).wait()
        for b in range(BATCH):
            level = jnp.full((1, 128), level_ref[0, 0, step, b].astype(F32), F32)
            sigma = 0.2 * jnp.exp(level * (math.log(25.0) / (LEVELS - 1)))
            c_in = 1.0 / jnp.sqrt(sigma * sigma + 0.25)

            def block(i, carry):
                at = pl.multiple_of(i * 128, 128)
                noisy = c_in * (
                    clean[step, b, :, pl.ds(at, 128)].astype(F32)
                    + sigma * noise[step, b, :, pl.ds(at, 128)].astype(F32)
                )
                x_ref[step, b, :, pl.ds(at, 128)] = noisy.astype(BF16)
                xt_ref[step, b, pl.ds(at, 128), :] = jnp.transpose(noisy).astype(BF16)
                return carry

            lax.fori_loop(0, CELLS // 128, block, 0)

    def exchange(step, chunk):
        return pltpu.make_async_remote_copy(
            src_ref=mine.at[step + 1, chunk],
            dst_ref=other.at[step + 1, chunk],
            send_sem=send_sem.at[step, chunk],
            recv_sem=recv_sem.at[step, chunk],
            device_id=partner_of(step),
            device_id_type=MESH,
        )

    def task(step, chunk):
        at = pl.multiple_of(chunk * OC, OC)

        @pl.when(step > 0)
        def _():
            exchange(step - 1, chunk).wait_recv()

        w = unpack(0.5 * (mine[step, chunk] + other[step, chunk]))
        square = jnp.sum(jnp.sum(w * w, axis=0), axis=1, keepdims=True)
        radius = jnp.sqrt(square / FAN + norm_epsilon)
        scale = 1.0 / (radius * math.sqrt(FAN))
        lhs = (w * scale).astype(BF16).reshape(TAPS * OC, C)
        grad_eff = jnp.zeros((TAPS * OC, C), F32)
        for b in range(BATCH):
            y = jnp.dot(lhs, x_ref[step, b], preferred_element_type=F32)
            tap = lambda dy, dx: y[(3 * (dy + 1) + dx + 1) * OC :][:OC]
            z = None
            for dx in (0, -1, 1):
                part = tap(0, dx)
                for dy in (-1, 1):
                    part = part + jnp.where(ok_row[dy], roll_cells(tap(dy, dx), -RES * dy), 0.0)
                z = part if dx == 0 else z + jnp.where(ok_col[dx], roll_cells(part, -dx), 0.0)
            sig = 1.0 / (1.0 + jnp.exp(-z))
            error = z * sig * (1.0 / silu_scale) - clean[step, b, pl.ds(at, OC), :].astype(F32)
            dz = error * sig * (1.0 + z * (1.0 - sig)) * (2.0 / (silu_scale * BATCH * CELLS))
            dz = dz.astype(BF16).astype(F32)
            pieces = {}
            for dx in (0, -1, 1):
                moved = dz if dx == 0 else roll_cells(jnp.where(ok_col[dx], dz, 0.0), dx)
                for dy in (0, -1, 1):
                    piece = (
                        moved if dy == 0 else roll_cells(jnp.where(ok_row[dy], moved, 0.0), RES * dy)
                    )
                    pieces[dy, dx] = piece.astype(BF16)
            rows = jnp.concatenate(
                [pieces[dy, dx] for dy in (-1, 0, 1) for dx in (-1, 0, 1)], axis=0
            )
            grad_eff += jnp.dot(rows, xt_ref[step, b], preferred_element_type=F32)
        grad_eff = grad_eff.reshape(TAPS, OC, C)
        inner = jnp.sum(jnp.sum(grad_eff * w, axis=0), axis=1, keepdims=True)
        back = inner / (FAN * math.sqrt(FAN) * (radius * radius * radius))
        grad = grad_eff * scale - w * back
        v = momentum_decay * vel[:, pl.ds(at, OC), :] + learn_rate * grad
        vel[:, pl.ds(at, OC), :] = v
        first, rest = pack(w - v)
        mine[step + 1, chunk, :, :OC, :] = first
        mine[step + 1, chunk, :, OC:, :] = rest
        exchange(step, chunk).start()

        @pl.when(step == STEPS - 1)
        def _():
            write(vel, new_v_hbm, 1, chunk).start()

    def write(src, dst, which, chunk):
        at = pl.multiple_of(chunk * OC, OC)
        return pltpu.make_async_copy(
            src.at[:, pl.ds(at, OC), :], dst.at[:, pl.ds(at, OC), :], out_sem.at[which, chunk]
        )

    def finish(chunk):
        at = pl.multiple_of(chunk * OC, OC)
        exchange(STEPS - 1, chunk).wait_recv()
        w_out[:, pl.ds(at, OC), :] = unpack(0.5 * (mine[STEPS, chunk] + other[STEPS, chunk]))
        write(w_out, new_w_hbm, 0, chunk).start()

    def wave(k, carry):
        @pl.when(k < STEPS)
        def _():
            prepare(k)

        def inner(step, carry):
            chunk = k - step - step // 2

            @pl.when((chunk >= 0) & (chunk < CHUNKS))
            def _():
                task(step, chunk)

            return carry

        lax.fori_loop(0, STEPS, inner, 0)

        @pl.when(k >= 5)
        def _():
            finish(k - 5)

        return carry

    lax.fori_loop(0, CHUNKS + 5, wave, 0)

    def drain(chunk, carry):
        for step in range(STEPS):
            exchange(step, chunk).wait_send()
        write(w_out, new_w_hbm, 0, chunk).wait()
        write(vel, new_v_hbm, 1, chunk).wait()
        return carry

    lax.fori_loop(0, CHUNKS, drain, 0)


def body(clean, noise, noise_level, weight, velocity):
    hbm = pl.BlockSpec(memory_space=pl.ANY)
    out = jax.ShapeDtypeStruct((TAPS, C, C), F32)
    new_w, new_v = pl.pallas_call(
        kernel,
        out_shape=(out, out),
        in_specs=[pl.BlockSpec(memory_space=pltpu.SMEM), hbm, hbm, hbm, hbm],
        out_specs=(hbm, hbm),
        scratch_shapes=[
            pltpu.VMEM((STEPS, BATCH, C, CELLS), BF16),
            pltpu.VMEM((STEPS, BATCH, C, CELLS), BF16),
            pltpu.VMEM((TAPS, C, C), F32),
            pltpu.VMEM((TAPS, C, C), F32),
            pltpu.VMEM((STEPS, BATCH, C, CELLS), BF16),
            pltpu.VMEM((STEPS, BATCH, CELLS, C), BF16),
            pltpu.VMEM((STEPS + 1, CHUNKS, TAPS, ROWS, 128), F32),
            pltpu.VMEM((STEPS + 1, CHUNKS, TAPS, ROWS, 128), F32),
            pltpu.VMEM((TAPS, C, C), F32),
            pltpu.VMEM((TAPS, C, C), F32),
            pltpu.VMEM((8, 128), F32),
            pltpu.SemaphoreType.DMA((2, STEPS)),
            pltpu.SemaphoreType.DMA((2,)),
            pltpu.SemaphoreType.DMA((2, CHUNKS)),
            pltpu.SemaphoreType.DMA((STEPS, CHUNKS)),
            pltpu.SemaphoreType.DMA((STEPS, CHUNKS)),
        ],
        compiler_params=pltpu.CompilerParams(
            collective_id=0, has_side_effects=True, vmem_limit_bytes=58 << 20
        ),
        name="train",
    )(noise_level, clean, noise, weight, velocity)
    return (
        jnp.swapaxes(new_w, 1, 2)[None, None],
        jnp.swapaxes(new_v, 1, 2)[None, None],
    )


def solution(mesh):
    in_specs = (
        P("rx", "ry", None, None, None, None),
        P("rx", "ry", None, None, None, None),
        P("rx", "ry", None, None),
        P("rx", "ry", None, None, None),
        P("rx", "ry", None, None, None),
    )
    out_specs = (P("rx", "ry", None, None, None), P("rx", "ry", None, None, None))
    return jax.shard_map(body, mesh=mesh, in_specs=in_specs, out_specs=out_specs, check_vma=False)
```

```python
import math

import jax
import jax.numpy as jnp
from jax import lax
from jax.experimental import pallas as pl
from jax.experimental.pallas import tpu as pltpu
from jax.sharding import PartitionSpec as P

RES = 32
CELLS = RES * RES
STEPS = 4
LEVELS = 32
C = 192
TAPS = 9
FAN = TAPS * C
OC = 16
HALF = OC // 2
ROWS = OC + HALF
UNITS = C // OC
CHUNKS = UNITS // 2 + 1
BATCH = 2
TILES = BATCH * CELLS // 128

norm_epsilon = 1e-05
momentum_decay = 0.9
learn_rate = 50.0
silu_scale = 0.596
MESH = pl.DeviceIdType.MESH
F32 = jnp.float32
BF16 = jnp.bfloat16


def partner_of(step):
    rx, ry = lax.axis_index("rx"), lax.axis_index("ry")
    odd = step % 2
    bit_x = (8 - 2 * step) * (1 - odd)
    bit_y = (10 - 2 * step) * odd
    px = rx + bit_x * (1 - 2 * ((rx // (bit_x + odd)) % 2))
    py = ry + bit_y * (1 - 2 * ((ry // (bit_y + 1 - odd)) % 2))
    return {"rx": px, "ry": py}


def pack(full):
    rest = full[:, :, 128:]
    return full[:, :, :128], jnp.concatenate([rest[:, :HALF], rest[:, HALF:]], axis=-1)


def unpack(packed):
    rest = packed[:, OC:]
    rest = jnp.concatenate([rest[:, :, :64], pltpu.roll(rest, 64, 2)[:, :, :64]], axis=1)
    return jnp.concatenate([packed[:, :OC], rest], axis=-1)


def kernel(
    level_ref, clean_hbm, noise_hbm, w_hbm, v_hbm, new_w_hbm, new_v_hbm,
    clean, noise, w_in, v_in, clean_p, x_ref, xt_ref, mine, other, vel, w_out,
    in_sem, wv_sem, out_sem, send_sem, recv_sem,
):
    pltpu.make_async_copy(w_hbm.at[0, 0], w_in, wv_sem.at[0]).start()
    pltpu.make_async_copy(v_hbm.at[0, 0], v_in, wv_sem.at[1]).start()
    for step in range(STEPS):
        pltpu.make_async_copy(clean_hbm.at[0, 0, step], clean.at[step], in_sem.at[0, step]).start()
        pltpu.make_async_copy(noise_hbm.at[0, 0, step], noise.at[step], in_sem.at[1, step]).start()

    barrier = pltpu.get_barrier_semaphore()
    for step in range(STEPS):
        pl.semaphore_signal(barrier, inc=1, device_id=partner_of(step), device_id_type=MESH)

    pltpu.make_async_copy(w_hbm.at[0, 0], w_in, wv_sem.at[0]).wait()
    pltpu.make_async_copy(v_hbm.at[0, 0], v_in, wv_sem.at[1]).wait()

    def turn(tap, carry):
        wt = jnp.transpose(w_in[tap])
        rest = wt[:, 128:].reshape(UNITS, 2, HALF, 64)
        rest = jnp.concatenate([rest[:, 0], rest[:, 1]], axis=-1)
        for slot in (mine, other):
            slot[0, :, tap, :OC, :] = wt[:, :128].reshape(UNITS, OC, 128)
            slot[0, :, tap, OC:, :] = rest
        vel[tap] = jnp.transpose(v_in[tap])
        return carry

    lax.fori_loop(0, TAPS, turn, 0)

    pl.semaphore_wait(barrier, STEPS)

    lane = lax.broadcasted_iota(jnp.int32, (1, 128), 1)
    low64, low32 = lane < 64, lane % 64 < 32
    col = lane % RES
    ok_col = {-1: col > 0, 1: col < RES - 1}
    ok_row = {-1: lane >= RES, 1: lane < 128 - RES}

    def regroup(tiles):
        out = [None] * 8
        for u in range(4):
            lo, hi = tiles[u], tiles[u + 4]
            out[u] = jnp.where(low64, lo, pltpu.roll(hi, 64, 1))
            out[u + 4] = jnp.where(low64, pltpu.roll(lo, 64, 1), hi)
        last = [None] * 8
        for high in range(2):
            for low in range(2):
                lo, hi = out[4 * high + low], out[4 * high + 2 + low]
                last[4 * low + 2 * high] = jnp.where(low32, lo, pltpu.roll(hi, 32, 1))
                last[4 * low + 2 * high + 1] = jnp.where(low32, pltpu.roll(lo, 96, 1), hi)
        return last

    def prepare(step):
        pltpu.make_async_copy(clean_hbm.at[0, 0, step], clean.at[step], in_sem.at[0, step]).wait()
        pltpu.make_async_copy(noise_hbm.at[0, 0, step], noise.at[step], in_sem.at[1, step]).wait()
        for b in range(BATCH):
            level = jnp.full((1, 128), level_ref[0, 0, b, step].astype(F32), F32)
            sigma = 0.2 * jnp.exp(level * (math.log(25.0) / (LEVELS - 1)))
            c_in = 1.0 / jnp.sqrt(sigma * sigma + 0.25)

            def block(i, carry):
                at = pl.ds(pl.multiple_of(i * 96, 96), 96)
                pair = [
                    regroup([ref[step, b, at, 128 * u : 128 * u + 128] for u in range(8)])
                    for ref in (clean, noise)
                ]
                for v in range(8):
                    to = 128 * (8 * b + v)
                    clean_p[step, at, to : to + 128] = pair[0][v]
                    noisy = c_in * (pair[0][v].astype(F32) + sigma * pair[1][v].astype(F32))
                    x_ref[step, at, to : to + 128] = noisy.astype(BF16)
                return carry

            lax.fori_loop(0, C // 96, block, 0)

        def turn_block(i, carry):
            at = pl.ds(pl.multiple_of(i * 128, 128), 128)
            xt_ref[step, at, :] = jnp.transpose(x_ref[step, :, at])
            return carry

        lax.fori_loop(0, TILES, turn_block, 0, unroll=True)

    def exchange(step, unit):
        return pltpu.make_async_remote_copy(
            src_ref=mine.at[step + 1, unit],
            dst_ref=other.at[step + 1, unit],
            send_sem=send_sem.at[step, unit],
            recv_sem=recv_sem.at[step, unit],
            device_id=partner_of(step),
            device_id_type=MESH,
        )

    def average(step, unit, units):
        both = [unpack(0.5 * (mine[step, unit + i] + other[step, unit + i])) for i in range(units)]
        return jnp.concatenate(both, axis=1)

    def task(step, unit, units):
        width = OC * units
        at = pl.ds(pl.multiple_of(unit * OC, OC), width)

        @pl.when(step > 0)
        def _():
            for i in range(units):
                exchange(step - 1, unit + i).wait_recv()

        w = average(step, unit, units)
        square = jnp.sum(jnp.sum(w * w, axis=0), axis=1, keepdims=True)
        radius = jnp.sqrt(square / FAN + norm_epsilon)
        scale = 1.0 / (radius * math.sqrt(FAN))
        lhs = (w * scale).astype(BF16).reshape(TAPS * width, C)
        y = jnp.dot(lhs, x_ref[step], preferred_element_type=F32)
        pieces = {}
        for b in range(BATCH):

            def tap(dy, dx, v):
                t, to = 3 * (dy + 1) + dx + 1, 128 * (8 * b + (v + dy) % 8)
                part = y[t * width : (t + 1) * width, to : to + 128]
                if 0 <= v + dy < 8:
                    return part
                return jnp.where(ok_row[dy], pltpu.roll(part, -RES * dy % 128, 1), 0.0)

            moved = {}
            for v in range(8):
                to = 128 * (8 * b + v)
                part = {dx: tap(0, dx, v) + tap(-1, dx, v) + tap(1, dx, v) for dx in (-1, 0, 1)}
                z = part[0]
                for dx in (-1, 1):
                    z = z + jnp.where(ok_col[dx], pltpu.roll(part[dx], -dx % 128, 1), 0.0)
                sig = 1.0 / (1.0 + jnp.exp(-z))
                error = z * sig * (1.0 / silu_scale) - clean_p[step, at, to : to + 128].astype(F32)
                dz = error * sig * (1.0 + z * (1.0 - sig)) * (2.0 / (silu_scale * BATCH * CELLS))
                moved[0, v] = dz = dz.astype(BF16)
                for dx in (-1, 1):
                    moved[dx, v] = jnp.where(
                        ok_col[-dx], pltpu.roll(dz, dx % 128, 1), jnp.zeros((), BF16)
                    )
            for v in range(8):
                for dx in (-1, 0, 1):
                    for dy in (-1, 0, 1):
                        piece = moved[dx, (v - dy) % 8]
                        if not 0 <= v - dy < 8:
                            piece = jnp.where(
                                ok_row[-dy], pltpu.roll(piece, RES * dy % 128, 1), jnp.zeros((), BF16)
                            )
                        pieces[dy, dx, 8 * b + v] = piece
        rows = jnp.concatenate(
            [
                jnp.concatenate([pieces[dy, dx, v] for v in range(TILES)], axis=1)
                for dy in (-1, 0, 1)
                for dx in (-1, 0, 1)
            ],
            axis=0,
        )
        grad_eff = jnp.dot(rows, xt_ref[step], preferred_element_type=F32)
        grad_eff = grad_eff.reshape(TAPS, width, C)
        inner = jnp.sum(jnp.sum(grad_eff * w, axis=0), axis=1, keepdims=True)
        back = inner / (FAN * math.sqrt(FAN) * (radius * radius * radius))
        grad = grad_eff * scale - w * back
        v = momentum_decay * vel[:, at, :] + learn_rate * grad
        vel[:, at, :] = v
        local = w - v
        for i in range(units):
            first, rest = pack(local[:, i * OC : (i + 1) * OC])
            mine[step + 1, unit + i, :, :OC, :] = first
            mine[step + 1, unit + i, :, OC:, :] = rest
            exchange(step, unit + i).start()

        @pl.when(step == STEPS - 1)
        def _():
            for i in range(units):
                write(vel, new_v_hbm, 1, unit + i).start()

    def write(src, dst, which, unit):
        at = pl.multiple_of(unit * OC, OC)
        return pltpu.make_async_copy(
            src.at[:, pl.ds(at, OC), :], dst.at[:, pl.ds(at, OC), :], out_sem.at[which, unit]
        )

    def finish(unit, units):
        for i in range(units):
            exchange(STEPS - 1, unit + i).wait_recv()
        w_out[:, pl.ds(pl.multiple_of(unit * OC, OC), OC * units), :] = average(STEPS, unit, units)
        for i in range(units):
            write(w_out, new_w_hbm, 0, unit + i).start()

    def on_chunk(chunk, do):
        unit = 2 * chunk - (chunk + CHUNKS - 1) // CHUNKS

        @pl.when((chunk == 0) | (chunk == CHUNKS - 1))
        def _():
            do(unit, 1)

        @pl.when((chunk > 0) & (chunk < CHUNKS - 1))
        def _():
            do(unit, 2)

    def wave(i, carry):
        k = i - 1

        def inner(step, carry):
            on_chunk(k - step - step // 2, lambda unit, units: task(step, unit, units))
            early = (step == 0) & (k == 1)
            late = (step == STEPS - 1) & ((k == -1) | (k == 1) | (k == 2))

            @pl.when(early | late)
            def _():
                prepare(k + step // (STEPS - 1))

            return carry

        lax.fori_loop(0, STEPS, inner, 0)
        on_chunk(k - 5, finish)
        return carry

    lax.fori_loop(0, CHUNKS + 6, wave, 0)

    def drain(unit, carry):
        for step in range(STEPS):
            exchange(step, unit).wait_send()
        write(w_out, new_w_hbm, 0, unit).wait()
        write(vel, new_v_hbm, 1, unit).wait()
        return carry

    lax.fori_loop(0, UNITS, drain, 0)


def body(clean, noise, noise_level, weight, velocity):
    hbm = pl.BlockSpec(memory_space=pl.ANY)
    out = jax.ShapeDtypeStruct((TAPS, C, C), F32)
    new_w, new_v = pl.pallas_call(
        kernel,
        out_shape=(out, out),
        in_specs=[pl.BlockSpec(memory_space=pltpu.SMEM), hbm, hbm, hbm, hbm],
        out_specs=(hbm, hbm),
        scratch_shapes=[
            pltpu.VMEM((STEPS, BATCH, C, CELLS), BF16),
            pltpu.VMEM((STEPS, BATCH, C, CELLS), BF16),
            pltpu.VMEM((TAPS, C, C), F32),
            pltpu.VMEM((TAPS, C, C), F32),
            pltpu.VMEM((STEPS, C, BATCH * CELLS), BF16),
            pltpu.VMEM((STEPS, C, BATCH * CELLS), BF16),
            pltpu.VMEM((STEPS, BATCH * CELLS, C), BF16),
            pltpu.VMEM((STEPS + 1, UNITS, TAPS, ROWS, 128), F32),
            pltpu.VMEM((STEPS + 1, UNITS, TAPS, ROWS, 128), F32),
            pltpu.VMEM((TAPS, C, C), F32),
            pltpu.VMEM((TAPS, C, C), F32),
            pltpu.SemaphoreType.DMA((2, STEPS)),
            pltpu.SemaphoreType.DMA((2,)),
            pltpu.SemaphoreType.DMA((2, UNITS)),
            pltpu.SemaphoreType.DMA((STEPS, UNITS)),
            pltpu.SemaphoreType.DMA((STEPS, UNITS)),
        ],
        compiler_params=pltpu.CompilerParams(
            collective_id=0, has_side_effects=True, vmem_limit_bytes=58 << 20
        ),
        name="train",
    )(jnp.swapaxes(noise_level, 2, 3), clean, noise, weight, velocity)
    return (
        jnp.swapaxes(new_w, 1, 2)[None, None],
        jnp.swapaxes(new_v, 1, 2)[None, None],
    )


def solution(mesh):
    in_specs = (
        P("rx", "ry", None, None, None, None),
        P("rx", "ry", None, None, None, None),
        P("rx", "ry", None, None),
        P("rx", "ry", None, None, None),
        P("rx", "ry", None, None, None),
    )
    out_specs = (P("rx", "ry", None, None, None), P("rx", "ry", None, None, None))
    return jax.shard_map(body, mesh=mesh, in_specs=in_specs, out_specs=out_specs, check_vma=False)
```

```python
import math

import jax
import jax.numpy as jnp
from jax import lax
from jax.experimental import pallas as pl
from jax.experimental.pallas import tpu as pltpu
from jax.sharding import PartitionSpec as P

RES = 32
CELLS = RES * RES
STEPS = 4
LEVELS = 32
C = 192
TAPS = 9
FAN = TAPS * C
OC = 16
HALF = OC // 2
ROWS = OC + HALF
UNITS = C // OC
DOUBLES = 4
CHUNKS = UNITS - DOUBLES
LAST_LAG = 6
BATCH = 2
TILES = BATCH * CELLS // 128

norm_epsilon = 1e-05
momentum_decay = 0.9
learn_rate = 50.0
silu_scale = 0.596
MESH = pl.DeviceIdType.MESH
F32 = jnp.float32
BF16 = jnp.bfloat16


def partner_of(step):
    rx, ry = lax.axis_index("rx"), lax.axis_index("ry")
    odd = step % 2
    bit_x = (8 - 2 * step) * (1 - odd)
    bit_y = (10 - 2 * step) * odd
    px = rx + bit_x * (1 - 2 * ((rx // (bit_x + odd)) % 2))
    py = ry + bit_y * (1 - 2 * ((ry // (bit_y + 1 - odd)) % 2))
    return {"rx": px, "ry": py}


def pack(full):
    rest = full[:, :, 128:]
    return full[:, :, :128], jnp.concatenate([rest[:, :HALF], rest[:, HALF:]], axis=-1)


def unpack(packed):
    rest = packed[:, OC:]
    rest = jnp.concatenate([rest[:, :, :64], pltpu.roll(rest, 64, 2)[:, :, :64]], axis=1)
    return jnp.concatenate([packed[:, :OC], rest], axis=-1)


def kernel(
    level_ref, clean_hbm, noise_hbm, w_hbm, v_hbm, new_w, new_v,
    clean, noise, w_in, v_in, clean_p, x_ref, xt_ref, mine, other, vel, w_out,
    in_sem, wv_sem, send_sem, recv_sem,
):
    def load(step):
        return (
            pltpu.make_async_copy(clean_hbm.at[0, 0, step], clean.at[step], in_sem.at[0, step]),
            pltpu.make_async_copy(noise_hbm.at[0, 0, step], noise.at[step], in_sem.at[1, step]),
        )

    load_w = pltpu.make_async_copy(w_hbm.at[0, 0], w_in, wv_sem.at[0])
    load_v = pltpu.make_async_copy(v_hbm.at[0, 0], v_in, wv_sem.at[1])
    for copy in load(0) + (load_w, load_v):
        copy.start()

    barrier = pltpu.get_barrier_semaphore()
    for step in range(STEPS):
        pl.semaphore_signal(barrier, inc=1, device_id=partner_of(step), device_id_type=MESH)

    def turn(tap, carry):
        wt = jnp.transpose(w_in[tap])
        rest = wt[:, 128:].reshape(UNITS, 2, HALF, 64)
        rest = jnp.concatenate([rest[:, 0], rest[:, 1]], axis=-1)
        for slot in (mine, other):
            slot[0, :, tap, :OC, :] = wt[:, :128].reshape(UNITS, OC, 128)
            slot[0, :, tap, OC:, :] = rest
        vel[tap] = jnp.transpose(v_in[tap])
        return carry

    lane = lax.broadcasted_iota(jnp.int32, (1, 128), 1)
    low64, low32 = lane < 64, lane % 64 < 32
    col = lane % RES
    ok_col = {-1: col > 0, 1: col < RES - 1}
    ok_row = {-1: lane >= RES, 1: lane < 128 - RES}

    def regroup(tiles):
        out = [None] * 8
        for u in range(4):
            lo, hi = tiles[u], tiles[u + 4]
            out[u] = jnp.where(low64, lo, pltpu.roll(hi, 64, 1))
            out[u + 4] = jnp.where(low64, pltpu.roll(lo, 64, 1), hi)
        last = [None] * 8
        for high in range(2):
            for low in range(2):
                lo, hi = out[4 * high + low], out[4 * high + 2 + low]
                last[4 * low + 2 * high] = jnp.where(low32, lo, pltpu.roll(hi, 32, 1))
                last[4 * low + 2 * high + 1] = jnp.where(low32, pltpu.roll(lo, 96, 1), hi)
        return last

    def prepare(step):
        for copy in load(step):
            copy.wait()
        for b in range(BATCH):
            level = jnp.full((1, 128), level_ref[0, 0, b, step].astype(F32), F32)
            sigma = 0.2 * jnp.exp(level * (math.log(25.0) / (LEVELS - 1)))
            c_in = 1.0 / jnp.sqrt(sigma * sigma + 0.25)

            pair = [
                regroup([ref[step, b, :, 128 * u : 128 * u + 128] for u in range(8)])
                for ref in (clean, noise)
            ]
            for v in range(8):
                to = 128 * (8 * b + v)
                clean_p[step, :, to : to + 128] = pair[0][v]
                noisy = c_in * (pair[0][v].astype(F32) + sigma * pair[1][v].astype(F32))
                x_ref[step, :, to : to + 128] = noisy.astype(BF16)

        def turn_block(i, carry):
            at = pl.ds(pl.multiple_of(i * 128, 128), 128)
            xt_ref[step, at, :] = jnp.transpose(x_ref[step, :, at])
            return carry

        lax.fori_loop(0, TILES, turn_block, 0, unroll=True)

    prepare(0)
    load_w.wait()
    load_v.wait()
    lax.fori_loop(0, TAPS, turn, 0, unroll=True)
    for step in range(1, STEPS):
        for copy in load(step):
            copy.start()
    pl.semaphore_wait(barrier, STEPS)

    def exchange(step, unit):
        return pltpu.make_async_remote_copy(
            src_ref=mine.at[step + 1, unit],
            dst_ref=other.at[step + 1, unit],
            send_sem=send_sem.at[step, unit],
            recv_sem=recv_sem.at[step, unit],
            device_id=partner_of(step),
            device_id_type=MESH,
        )

    def average(step, unit, units):
        both = [unpack(0.5 * (mine[step, unit + i] + other[step, unit + i])) for i in range(units)]
        return jnp.concatenate(both, axis=1)

    def task(step, unit, units):
        width = OC * units
        at = pl.ds(pl.multiple_of(unit * OC, OC), width)

        @pl.when(step > 0)
        def _():
            for i in range(units):
                exchange(step - 1, unit + i).wait_recv()

        w = average(step, unit, units)
        square = jnp.sum(jnp.sum(w * w, axis=0), axis=1, keepdims=True)
        radius = jnp.sqrt(square / FAN + norm_epsilon)
        scale = 1.0 / (radius * math.sqrt(FAN))
        lhs = (w * scale).astype(BF16).reshape(TAPS * width, C)
        y = jnp.dot(lhs, x_ref[step], preferred_element_type=F32)
        pieces = {}
        for b in range(BATCH):

            def tap(dy, dx, v):
                t, to = 3 * (dy + 1) + dx + 1, 128 * (8 * b + (v + dy) % 8)
                part = y[t * width : (t + 1) * width, to : to + 128]
                if 0 <= v + dy < 8:
                    return part
                return jnp.where(ok_row[dy], pltpu.roll(part, -RES * dy % 128, 1), 0.0)

            moved = {}
            for v in range(8):
                to = 128 * (8 * b + v)
                part = {dx: tap(0, dx, v) + tap(-1, dx, v) + tap(1, dx, v) for dx in (-1, 0, 1)}
                z = part[0]
                for dx in (-1, 1):
                    z = z + jnp.where(ok_col[dx], pltpu.roll(part[dx], -dx % 128, 1), 0.0)
                sig = 1.0 / (1.0 + jnp.exp(-z))
                error = z * sig * (1.0 / silu_scale) - clean_p[step, at, to : to + 128].astype(F32)
                dz = error * sig * (1.0 + z * (1.0 - sig)) * (2.0 / (silu_scale * BATCH * CELLS))
                moved[0, v] = dz = dz.astype(BF16)
                for dx in (-1, 1):
                    moved[dx, v] = jnp.where(
                        ok_col[-dx], pltpu.roll(dz, dx % 128, 1), jnp.zeros((), BF16)
                    )
            for v in range(8):
                for dx in (-1, 0, 1):
                    for dy in (-1, 0, 1):
                        piece = moved[dx, (v - dy) % 8]
                        if not 0 <= v - dy < 8:
                            piece = jnp.where(
                                ok_row[-dy], pltpu.roll(piece, RES * dy % 128, 1), jnp.zeros((), BF16)
                            )
                        pieces[dy, dx, 8 * b + v] = piece
        rows = jnp.concatenate(
            [
                jnp.concatenate([pieces[dy, dx, v] for v in range(TILES)], axis=1)
                for dy in (-1, 0, 1)
                for dx in (-1, 0, 1)
            ],
            axis=0,
        )
        grad_eff = jnp.dot(rows, xt_ref[step], preferred_element_type=F32)
        grad_eff = grad_eff.reshape(TAPS, width, C)
        inner = jnp.sum(jnp.sum(grad_eff * w, axis=0), axis=1, keepdims=True)
        back = inner / (FAN * math.sqrt(FAN) * (radius * radius * radius))
        grad = grad_eff * scale - w * back
        v = momentum_decay * vel[:, at, :] + learn_rate * grad
        vel[:, at, :] = v
        local = w - v
        for i in range(units):
            first, rest = pack(local[:, i * OC : (i + 1) * OC])
            mine[step + 1, unit + i, :, :OC, :] = first
            mine[step + 1, unit + i, :, OC:, :] = rest
            exchange(step, unit + i).start()

    def finish(unit, units):
        for i in range(units):
            exchange(STEPS - 1, unit + i).wait_recv()
        w_out[:, pl.ds(pl.multiple_of(unit * OC, OC), OC * units), :] = average(STEPS, unit, units)

    def on_chunk(chunk, do):
        unit = jnp.minimum(2 * chunk - (chunk + CHUNKS - 1) // CHUNKS, chunk + DOUBLES)

        @pl.when((chunk == 0) | ((chunk > DOUBLES) & (chunk < CHUNKS)))
        def _():
            do(unit, 1)

        @pl.when((chunk > 0) & (chunk <= DOUBLES))
        def _():
            do(unit, 2)

    def wave(k, carry):
        def inner(step, carry):
            chunk = k - step - step // 2

            @pl.when((chunk == 0) & (step > 0))
            def _():
                prepare(step)

            on_chunk(chunk, lambda unit, units: task(step, unit, units))
            return carry

        lax.fori_loop(0, STEPS, inner, 0)

        @pl.when(k == CHUNKS + LAST_LAG - 2)
        def _():
            def turn_back(tap, carry):
                new_v[tap] = jnp.transpose(vel[tap])
                new_w[tap, :, :128] = jnp.transpose(w_out[tap, :128])
                return carry

            lax.fori_loop(0, TAPS, turn_back, 0)

        on_chunk(k - LAST_LAG, finish)
        return carry

    lax.fori_loop(0, CHUNKS + LAST_LAG, wave, 0)

    def turn_rest(tap, carry):
        new_w[tap, :, 128:] = jnp.transpose(w_out[tap, 128:])
        return carry

    lax.fori_loop(0, TAPS, turn_rest, 0, unroll=True)

    def drain(unit, carry):
        for step in range(STEPS):
            exchange(step, unit).wait_send()
        return carry

    lax.fori_loop(0, UNITS, drain, 0)


def body(clean, noise, noise_level, weight, velocity):
    hbm = pl.BlockSpec(memory_space=pl.ANY)
    out = pltpu.VMEM((TAPS, C, C), F32)
    vmem = pl.BlockSpec(memory_space=pltpu.VMEM)
    new_w, new_v = pl.pallas_call(
        kernel,
        out_shape=(out, out),
        in_specs=[pl.BlockSpec(memory_space=pltpu.SMEM), hbm, hbm, hbm, hbm],
        out_specs=(vmem, vmem),
        scratch_shapes=[
            pltpu.VMEM((STEPS, BATCH, C, CELLS), BF16),
            pltpu.VMEM((STEPS, BATCH, C, CELLS), BF16),
            pltpu.VMEM((TAPS, C, C), F32),
            pltpu.VMEM((TAPS, C, C), F32),
            pltpu.VMEM((STEPS, C, BATCH * CELLS), BF16),
            pltpu.VMEM((STEPS, C, BATCH * CELLS), BF16),
            pltpu.VMEM((STEPS, BATCH * CELLS, C), BF16),
            pltpu.VMEM((STEPS + 1, UNITS, TAPS, ROWS, 128), F32),
            pltpu.VMEM((STEPS + 1, UNITS, TAPS, ROWS, 128), F32),
            pltpu.VMEM((TAPS, C, C), F32),
            pltpu.VMEM((TAPS, C, C), F32),
            pltpu.SemaphoreType.DMA((2, STEPS)),
            pltpu.SemaphoreType.DMA((2,)),
            pltpu.SemaphoreType.DMA((STEPS, UNITS)),
            pltpu.SemaphoreType.DMA((STEPS, UNITS)),
        ],
        compiler_params=pltpu.CompilerParams(
            collective_id=0, has_side_effects=True, vmem_limit_bytes=52 << 20
        ),
        name="train",
    )(jnp.swapaxes(noise_level, 2, 3), clean, noise, weight, velocity)
    return (new_w[None, None], new_v[None, None])


def solution(mesh):
    in_specs = (
        P("rx", "ry", None, None, None, None),
        P("rx", "ry", None, None, None, None),
        P("rx", "ry", None, None),
        P("rx", "ry", None, None, None),
        P("rx", "ry", None, None, None),
    )
    out_specs = (P("rx", "ry", None, None, None), P("rx", "ry", None, None, None))
    return jax.shard_map(body, mesh=mesh, in_specs=in_specs, out_specs=out_specs, check_vma=False)
```

```python
import math

import jax
import jax.numpy as jnp
from jax import lax
from jax.experimental import pallas as pl
from jax.experimental.pallas import tpu as pltpu
from jax.sharding import PartitionSpec as P

RES = 32
CELLS = RES * RES
STEPS = 4
LEVELS = 32
C = 192
TAPS = 9
FAN = TAPS * C
OC = 16
HALF = OC // 2
ROWS = OC + HALF
UNITS = C // OC
DOUBLES = 4
CHUNKS = UNITS - DOUBLES
LAST_LAG = 6
BATCH = 2
TILES = BATCH * CELLS // 128

norm_epsilon = 1e-05
momentum_decay = 0.9
learn_rate = 50.0
silu_scale = 0.596
MESH = pl.DeviceIdType.MESH
F32 = jnp.float32
BF16 = jnp.bfloat16


def partner_of(step):
    rx, ry = lax.axis_index("rx"), lax.axis_index("ry")
    odd = step % 2
    bit_x = (8 - 2 * step) * (1 - odd)
    bit_y = (10 - 2 * step) * odd
    px = rx + bit_x * (1 - 2 * ((rx // (bit_x + odd)) % 2))
    py = ry + bit_y * (1 - 2 * ((ry // (bit_y + 1 - odd)) % 2))
    return {"rx": px, "ry": py}


def pack(full):
    rest = full[:, :, 128:]
    return full[:, :, :128], jnp.concatenate([rest[:, :HALF], rest[:, HALF:]], axis=-1)


def unpack(packed):
    rest = packed[:, OC:]
    rest = jnp.concatenate([rest[:, :, :64], pltpu.roll(rest, 64, 2)[:, :, :64]], axis=1)
    return jnp.concatenate([packed[:, :OC], rest], axis=-1)


def kernel(
    level_ref, clean_hbm, noise_hbm, w_hbm, v_hbm, new_w, new_v,
    clean, noise, w_in, v_in, clean_p, x_ref, xt_ref, mine, other, vel, w_out,
    in_sem, wv_sem, send_sem, recv_sem,
):
    def load(step):
        return (
            pltpu.make_async_copy(clean_hbm.at[0, 0, step], clean.at[step], in_sem.at[0, step]),
            pltpu.make_async_copy(noise_hbm.at[0, 0, step], noise.at[step], in_sem.at[1, step]),
        )

    load_w = pltpu.make_async_copy(w_hbm.at[0, 0], w_in, wv_sem.at[0])
    load_v = pltpu.make_async_copy(v_hbm.at[0, 0], v_in, wv_sem.at[1])
    for copy in load(0) + (load_w, load_v):
        copy.start()

    barrier = pltpu.get_barrier_semaphore()
    for step in range(STEPS):
        pl.semaphore_signal(barrier, inc=1, device_id=partner_of(step), device_id_type=MESH)

    def turn(tap, carry):
        wt = jnp.transpose(w_in[tap])
        rest = wt[:, 128:].reshape(UNITS, 2, HALF, 64)
        rest = jnp.concatenate([rest[:, 0], rest[:, 1]], axis=-1)
        for slot in (mine, other):
            slot[0, :, tap, :OC, :] = wt[:, :128].reshape(UNITS, OC, 128)
            slot[0, :, tap, OC:, :] = rest
        vel[tap] = jnp.transpose(v_in[tap])
        return carry

    lane = lax.broadcasted_iota(jnp.int32, (1, 128), 1)
    low64, low32 = lane < 64, lane % 64 < 32
    col = lane % RES
    ok_col = {-1: col > 0, 1: col < RES - 1}
    ok_row = {-1: lane >= RES, 1: lane < 128 - RES}

    def regroup(tiles):
        out = [None] * 8
        for u in range(4):
            lo, hi = tiles[u], tiles[u + 4]
            out[u] = jnp.where(low64, lo, pltpu.roll(hi, 64, 1))
            out[u + 4] = jnp.where(low64, pltpu.roll(lo, 64, 1), hi)
        last = [None] * 8
        for high in range(2):
            for low in range(2):
                lo, hi = out[4 * high + low], out[4 * high + 2 + low]
                last[4 * low + 2 * high] = jnp.where(low32, lo, pltpu.roll(hi, 32, 1))
                last[4 * low + 2 * high + 1] = jnp.where(low32, pltpu.roll(lo, 96, 1), hi)
        return last

    def prepare(step):
        for copy in load(step):
            copy.wait()
        for b in range(BATCH):
            level = jnp.full((1, 128), level_ref[0, 0, b, step].astype(F32), F32)
            sigma = 0.2 * jnp.exp(level * (math.log(25.0) / (LEVELS - 1)))
            c_in = 1.0 / jnp.sqrt(sigma * sigma + 0.25)

            pair = [
                regroup([ref[step, b, :, 128 * u : 128 * u + 128] for u in range(8)])
                for ref in (clean, noise)
            ]
            for v in range(8):
                to = 128 * (8 * b + v)
                clean_p[step, :, to : to + 128] = pair[0][v]
                noisy = c_in * (pair[0][v].astype(F32) + sigma * pair[1][v].astype(F32))
                x_ref[step, :, to : to + 128] = noisy.astype(BF16)

        def turn_block(i, carry):
            at = pl.ds(pl.multiple_of(i * 128, 128), 128)
            xt_ref[step, at, :] = jnp.transpose(x_ref[step, :, at])
            return carry

        lax.fori_loop(0, TILES, turn_block, 0, unroll=True)

    prepare(0)
    load_w.wait()
    load_v.wait()
    lax.fori_loop(0, TAPS, turn, 0, unroll=True)
    for step in range(1, STEPS):
        for copy in load(step):
            copy.start()
    pl.semaphore_wait(barrier, STEPS)

    def exchange(step, unit):
        return pltpu.make_async_remote_copy(
            src_ref=mine.at[step + 1, unit],
            dst_ref=other.at[step + 1, unit],
            send_sem=send_sem.at[step, unit],
            recv_sem=recv_sem.at[step, unit],
            device_id=partner_of(step),
            device_id_type=MESH,
        )

    def average(step, unit, units):
        both = [unpack(0.5 * (mine[step, unit + i] + other[step, unit + i])) for i in range(units)]
        return jnp.concatenate(both, axis=1)

    def task(step, unit, units):
        width = OC * units
        at = pl.ds(pl.multiple_of(unit * OC, OC), width)

        @pl.when(step > 0)
        def _():
            for i in range(units):
                exchange(step - 1, unit + i).wait_recv()

        w = average(step, unit, units)
        square = jnp.sum(jnp.sum(w * w, axis=0), axis=1, keepdims=True)
        radius = jnp.sqrt(square / FAN + norm_epsilon)
        scale = 1.0 / (radius * math.sqrt(FAN))
        lhs = (w * scale).astype(BF16).reshape(TAPS * width, C)
        y = jnp.dot(lhs, x_ref[step], preferred_element_type=F32)
        pieces = {}
        for b in range(BATCH):

            def tap(dy, dx, v):
                t, to = 3 * (dy + 1) + dx + 1, 128 * (8 * b + (v + dy) % 8)
                part = y[t * width : (t + 1) * width, to : to + 128]
                if 0 <= v + dy < 8:
                    return part
                return jnp.where(ok_row[dy], pltpu.roll(part, -RES * dy % 128, 1), 0.0)

            moved = {}
            for v in range(8):
                to = 128 * (8 * b + v)
                part = {dx: tap(0, dx, v) + tap(-1, dx, v) + tap(1, dx, v) for dx in (-1, 0, 1)}
                z = part[0]
                for dx in (-1, 1):
                    z = z + jnp.where(ok_col[dx], pltpu.roll(part[dx], -dx % 128, 1), 0.0)
                sig = 1.0 / (1.0 + jnp.exp(-z))
                error = z * sig * (1.0 / silu_scale) - clean_p[step, at, to : to + 128].astype(F32)
                dz = error * sig * (1.0 + z * (1.0 - sig)) * (2.0 / (silu_scale * BATCH * CELLS))
                moved[0, v] = dz = dz.astype(BF16)
                for dx in (-1, 1):
                    moved[dx, v] = jnp.where(
                        ok_col[-dx], pltpu.roll(dz, dx % 128, 1), jnp.zeros((), BF16)
                    )
            for v in range(8):
                for dx in (-1, 0, 1):
                    for dy in (-1, 0, 1):
                        piece = moved[dx, (v - dy) % 8]
                        if not 0 <= v - dy < 8:
                            piece = jnp.where(
                                ok_row[-dy], pltpu.roll(piece, RES * dy % 128, 1), jnp.zeros((), BF16)
                            )
                        pieces[dy, dx, 8 * b + v] = piece
        rows = jnp.concatenate(
            [
                jnp.concatenate([pieces[dy, dx, v] for v in range(TILES)], axis=1)
                for dy in (-1, 0, 1)
                for dx in (-1, 0, 1)
            ],
            axis=0,
        )
        grad_eff = jnp.dot(rows, xt_ref[step], preferred_element_type=F32)
        grad_eff = grad_eff.reshape(TAPS, width, C)
        inner = jnp.sum(jnp.sum(grad_eff * w, axis=0), axis=1, keepdims=True)
        back = inner / (FAN * math.sqrt(FAN) * (radius * radius * radius))
        grad = grad_eff * scale - w * back
        v = momentum_decay * vel[:, at, :] + learn_rate * grad
        vel[:, at, :] = v
        local = w - v
        for i in range(units):
            first, rest = pack(local[:, i * OC : (i + 1) * OC])
            mine[step + 1, unit + i, :, :OC, :] = first
            mine[step + 1, unit + i, :, OC:, :] = rest
            exchange(step, unit + i).start()

    def finish(unit, units):
        for i in range(units):
            exchange(STEPS - 1, unit + i).wait_recv()
        w_out[:, pl.ds(pl.multiple_of(unit * OC, OC), OC * units), :] = average(STEPS, unit, units)

    def on_chunk(chunk, do):
        unit = jnp.minimum(2 * chunk - (chunk + CHUNKS - 1) // CHUNKS, chunk + DOUBLES)

        @pl.when((chunk == 0) | ((chunk > DOUBLES) & (chunk < CHUNKS)))
        def _():
            do(unit, 1)

        @pl.when((chunk > 0) & (chunk <= DOUBLES))
        def _():
            do(unit, 2)

    def drain(unit, carry):
        for step in range(STEPS):
            exchange(step, unit).wait_send()
        return carry

    def wave(k, carry):
        def inner(step, carry):
            chunk = k - step - step // 2

            @pl.when((chunk == 0) & (step > 0))
            def _():
                prepare(step)

            on_chunk(chunk, lambda unit, units: task(step, unit, units))
            return carry

        lax.fori_loop(0, STEPS, inner, 0)

        @pl.when(k == CHUNKS + LAST_LAG - 2)
        def _():
            def turn_back(tap, carry):
                new_v[tap] = jnp.transpose(vel[tap])
                new_w[tap, :, :128] = jnp.transpose(w_out[tap, :128])
                return carry

            lax.fori_loop(0, TAPS, turn_back, 0)

        @pl.when(k == CHUNKS + LAST_LAG - 1)
        def _():
            lax.fori_loop(0, UNITS, drain, 0)

        on_chunk(k - LAST_LAG, finish)
        return carry

    lax.fori_loop(0, CHUNKS + LAST_LAG, wave, 0)

    def turn_rest(tap, carry):
        new_w[tap, :, 128:] = jnp.transpose(w_out[tap, 128:])
        return carry

    lax.fori_loop(0, TAPS, turn_rest, 0, unroll=True)


def store(new_w, new_v, w_hbm, v_hbm, sem):
    copies = (
        pltpu.make_async_copy(new_w, w_hbm.at[0, 0], sem.at[0]),
        pltpu.make_async_copy(new_v, v_hbm.at[0, 0], sem.at[1]),
    )
    for copy in copies:
        copy.start()
    for copy in copies:
        copy.wait()


def body(clean, noise, noise_level, weight, velocity):
    hbm = pl.BlockSpec(memory_space=pl.ANY)
    out = pltpu.VMEM((TAPS, C, C), F32)
    vmem = pl.BlockSpec(memory_space=pltpu.VMEM)
    new_w, new_v = pl.pallas_call(
        kernel,
        out_shape=(out, out),
        in_specs=[pl.BlockSpec(memory_space=pltpu.SMEM), hbm, hbm, hbm, hbm],
        out_specs=(vmem, vmem),
        scratch_shapes=[
            pltpu.VMEM((STEPS, BATCH, C, CELLS), BF16),
            pltpu.VMEM((STEPS, BATCH, C, CELLS), BF16),
            pltpu.VMEM((TAPS, C, C), F32),
            pltpu.VMEM((TAPS, C, C), F32),
            pltpu.VMEM((STEPS, C, BATCH * CELLS), BF16),
            pltpu.VMEM((STEPS, C, BATCH * CELLS), BF16),
            pltpu.VMEM((STEPS, BATCH * CELLS, C), BF16),
            pltpu.VMEM((STEPS + 1, UNITS, TAPS, ROWS, 128), F32),
            pltpu.VMEM((STEPS + 1, UNITS, TAPS, ROWS, 128), F32),
            pltpu.VMEM((TAPS, C, C), F32),
            pltpu.VMEM((TAPS, C, C), F32),
            pltpu.SemaphoreType.DMA((2, STEPS)),
            pltpu.SemaphoreType.DMA((2,)),
            pltpu.SemaphoreType.DMA((STEPS, UNITS)),
            pltpu.SemaphoreType.DMA((STEPS, UNITS)),
        ],
        compiler_params=pltpu.CompilerParams(
            collective_id=0, has_side_effects=True, vmem_limit_bytes=52 << 20
        ),
        name="train",
    )(jnp.swapaxes(noise_level, 2, 3), clean, noise, weight, velocity)
    shape = jax.ShapeDtypeStruct((1, 1, TAPS, C, C), F32)
    return pl.pallas_call(
        store,
        out_shape=(shape, shape),
        in_specs=[vmem, vmem],
        out_specs=(hbm, hbm),
        scratch_shapes=[pltpu.SemaphoreType.DMA((2,))],
        name="store",
    )(pltpu.with_memory_space_constraint(new_w, pltpu.VMEM), pltpu.with_memory_space_constraint(new_v, pltpu.VMEM))


def solution(mesh):
    in_specs = (
        P("rx", "ry", None, None, None, None),
        P("rx", "ry", None, None, None, None),
        P("rx", "ry", None, None),
        P("rx", "ry", None, None, None),
        P("rx", "ry", None, None, None),
    )
    out_specs = (P("rx", "ry", None, None, None), P("rx", "ry", None, None, None))
    return jax.shard_map(body, mesh=mesh, in_specs=in_specs, out_specs=out_specs, check_vma=False)
```

```python
import math

import jax
import jax.numpy as jnp
from jax import lax
from jax.experimental import pallas as pl
from jax.experimental.pallas import tpu as pltpu
from jax.sharding import PartitionSpec as P

RES = 32
CELLS = RES * RES
STEPS = 4
LEVELS = 32
C = 192
TAPS = 9
FAN = TAPS * C
OC = 16
HALF = OC // 2
ROWS = OC + HALF
UNITS = C // OC
DOUBLES = 4
CHUNKS = UNITS - DOUBLES
LAST_LAG = 6
BATCH = 2
TILES = BATCH * CELLS // 128

norm_epsilon = 1e-05
momentum_decay = 0.9
learn_rate = 50.0
silu_scale = 0.596
MESH = pl.DeviceIdType.MESH
F32 = jnp.float32
BF16 = jnp.bfloat16


def partner_of(step):
    rx, ry = lax.axis_index("rx"), lax.axis_index("ry")
    odd = step % 2
    bit_x = (8 - 2 * step) * (1 - odd)
    bit_y = (10 - 2 * step) * odd
    px = rx + bit_x * (1 - 2 * ((rx // (bit_x + odd)) % 2))
    py = ry + bit_y * (1 - 2 * ((ry // (bit_y + 1 - odd)) % 2))
    return {"rx": px, "ry": py}


def pack(full):
    rest = full[:, :, 128:]
    return full[:, :, :128], jnp.concatenate([rest[:, :HALF], rest[:, HALF:]], axis=-1)


def unpack(packed):
    rest = packed[:, OC:]
    rest = jnp.concatenate([rest[:, :, :64], pltpu.roll(rest, 64, 2)[:, :, :64]], axis=1)
    return jnp.concatenate([packed[:, :OC], rest], axis=-1)


def kernel(
    level_ref, clean_hbm, noise_hbm, w_hbm, v_hbm, new_w, new_v,
    clean, noise, w_in, v_in, clean_p, x_ref, xt_ref, mine, other, vel, w_out,
    in_sem, wv_sem, send_sem, recv_sem,
):
    def load(step):
        return (
            pltpu.make_async_copy(clean_hbm.at[0, 0, step], clean.at[step], in_sem.at[0, step]),
            pltpu.make_async_copy(noise_hbm.at[0, 0, step], noise.at[step], in_sem.at[1, step]),
        )

    load_w = pltpu.make_async_copy(w_hbm.at[0, 0], w_in, wv_sem.at[0])
    load_v = pltpu.make_async_copy(v_hbm.at[0, 0], v_in, wv_sem.at[1])
    for copy in load(0) + (load_w, load_v):
        copy.start()

    barrier = pltpu.get_barrier_semaphore()
    for step in range(STEPS):
        pl.semaphore_signal(barrier, inc=1, device_id=partner_of(step), device_id_type=MESH)

    def turn(tap, carry):
        wt = jnp.transpose(w_in[tap])
        rest = wt[:, 128:].reshape(UNITS, 2, HALF, 64)
        rest = jnp.concatenate([rest[:, 0], rest[:, 1]], axis=-1)
        for slot in (mine, other):
            slot[0, :, tap, :OC, :] = wt[:, :128].reshape(UNITS, OC, 128)
            slot[0, :, tap, OC:, :] = rest
        vel[tap] = jnp.transpose(v_in[tap])
        return carry

    lane = lax.broadcasted_iota(jnp.int32, (1, 128), 1)
    low64, low32 = lane < 64, lane % 64 < 32
    col = lane % RES
    ok_col = {-1: col > 0, 1: col < RES - 1}
    ok_row = {-1: lane >= RES, 1: lane < 128 - RES}

    def regroup(tiles):
        out = [None] * 8
        for u in range(4):
            lo, hi = tiles[u], tiles[u + 4]
            out[u] = jnp.where(low64, lo, pltpu.roll(hi, 64, 1))
            out[u + 4] = jnp.where(low64, pltpu.roll(lo, 64, 1), hi)
        last = [None] * 8
        for high in range(2):
            for low in range(2):
                lo, hi = out[4 * high + low], out[4 * high + 2 + low]
                last[4 * low + 2 * high] = jnp.where(low32, lo, pltpu.roll(hi, 32, 1))
                last[4 * low + 2 * high + 1] = jnp.where(low32, pltpu.roll(lo, 96, 1), hi)
        return last

    def prepare(step):
        for copy in load(step):
            copy.wait()
        for b in range(BATCH):
            level = jnp.full((1, 128), level_ref[0, 0, b, step].astype(F32), F32)
            sigma = 0.2 * jnp.exp(level * (math.log(25.0) / (LEVELS - 1)))
            c_in = 1.0 / jnp.sqrt(sigma * sigma + 0.25)

            pair = [
                regroup([ref[step, b, :, 128 * u : 128 * u + 128] for u in range(8)])
                for ref in (clean, noise)
            ]
            for v in range(8):
                to = 128 * (8 * b + v)
                clean_p[step, :, to : to + 128] = pair[0][v]
                noisy = c_in * (pair[0][v].astype(F32) + sigma * pair[1][v].astype(F32))
                x_ref[step, :, to : to + 128] = noisy.astype(BF16)

    def turn_inputs(step):
        def turn_block(i, carry):
            at = pl.ds(pl.multiple_of(i * 128, 128), 128)
            xt_ref[step, at, :] = jnp.transpose(x_ref[step, :, at])
            return carry

        lax.fori_loop(0, TILES, turn_block, 0, unroll=True)

    prepare(0)
    load_w.wait()
    load_v.wait()
    turn_inputs(0)
    lax.fori_loop(0, TAPS, turn, 0, unroll=True)
    for step in range(1, STEPS):
        for copy in load(step):
            copy.start()
    pl.semaphore_wait(barrier, STEPS)

    def exchange(step, unit):
        return pltpu.make_async_remote_copy(
            src_ref=mine.at[step + 1, unit],
            dst_ref=other.at[step + 1, unit],
            send_sem=send_sem.at[step, unit],
            recv_sem=recv_sem.at[step, unit],
            device_id=partner_of(step),
            device_id_type=MESH,
        )

    def average(step, unit, units):
        both = [unpack(0.5 * (mine[step, unit + i] + other[step, unit + i])) for i in range(units)]
        return jnp.concatenate(both, axis=1)

    def task(step, unit, units):
        width = OC * units
        at = pl.ds(pl.multiple_of(unit * OC, OC), width)

        @pl.when(step > 0)
        def _():
            for i in range(units):
                exchange(step - 1, unit + i).wait_recv()

        w = average(step, unit, units)
        square = jnp.sum(jnp.sum(w * w, axis=0), axis=1, keepdims=True)
        radius = jnp.sqrt(square / FAN + norm_epsilon)
        scale = 1.0 / (radius * math.sqrt(FAN))
        lhs = (w * scale).astype(BF16).reshape(TAPS * width, C)
        y = jnp.dot(lhs, x_ref[step], preferred_element_type=F32)
        pieces = {}
        for b in range(BATCH):

            def tap(dy, dx, v):
                t, to = 3 * (dy + 1) + dx + 1, 128 * (8 * b + (v + dy) % 8)
                part = y[t * width : (t + 1) * width, to : to + 128]
                if 0 <= v + dy < 8:
                    return part
                return jnp.where(ok_row[dy], pltpu.roll(part, -RES * dy % 128, 1), 0.0)

            moved = {}
            for v in range(8):
                to = 128 * (8 * b + v)
                part = {dx: tap(0, dx, v) + tap(-1, dx, v) + tap(1, dx, v) for dx in (-1, 0, 1)}
                z = part[0]
                for dx in (-1, 1):
                    z = z + jnp.where(ok_col[dx], pltpu.roll(part[dx], -dx % 128, 1), 0.0)
                sig = 1.0 / (1.0 + jnp.exp(-z))
                error = z * sig * (1.0 / silu_scale) - clean_p[step, at, to : to + 128].astype(F32)
                dz = error * sig * (1.0 + z * (1.0 - sig)) * (2.0 / (silu_scale * BATCH * CELLS))
                moved[0, v] = dz = dz.astype(BF16)
                for dx in (-1, 1):
                    moved[dx, v] = jnp.where(
                        ok_col[-dx], pltpu.roll(dz, dx % 128, 1), jnp.zeros((), BF16)
                    )
            for v in range(8):
                for dx in (-1, 0, 1):
                    for dy in (-1, 0, 1):
                        piece = moved[dx, (v - dy) % 8]
                        if not 0 <= v - dy < 8:
                            piece = jnp.where(
                                ok_row[-dy], pltpu.roll(piece, RES * dy % 128, 1), jnp.zeros((), BF16)
                            )
                        pieces[dy, dx, 8 * b + v] = piece
        rows = jnp.concatenate(
            [
                jnp.concatenate([pieces[dy, dx, v] for v in range(TILES)], axis=1)
                for dy in (-1, 0, 1)
                for dx in (-1, 0, 1)
            ],
            axis=0,
        )
        grad_eff = jnp.dot(rows, xt_ref[step], preferred_element_type=F32)
        grad_eff = grad_eff.reshape(TAPS, width, C)
        inner = jnp.sum(jnp.sum(grad_eff * w, axis=0), axis=1, keepdims=True)
        back = inner / (FAN * math.sqrt(FAN) * (radius * radius * radius))
        grad = grad_eff * scale - w * back
        v = momentum_decay * vel[:, at, :] + learn_rate * grad
        vel[:, at, :] = v
        local = w - v
        for i in range(units):
            first, rest = pack(local[:, i * OC : (i + 1) * OC])
            mine[step + 1, unit + i, :, :OC, :] = first
            mine[step + 1, unit + i, :, OC:, :] = rest
            exchange(step, unit + i).start()

    def finish(unit, units):
        for i in range(units):
            exchange(STEPS - 1, unit + i).wait_recv()
        w_out[:, pl.ds(pl.multiple_of(unit * OC, OC), OC * units), :] = average(STEPS, unit, units)

    def on_chunk(chunk, do):
        unit = jnp.minimum(2 * chunk - (chunk + CHUNKS - 1) // CHUNKS, chunk + DOUBLES)

        @pl.when((chunk == 0) | ((chunk > DOUBLES) & (chunk < CHUNKS)))
        def _():
            do(unit, 1)

        @pl.when((chunk > 0) & (chunk <= DOUBLES))
        def _():
            do(unit, 2)

    def drain(unit, carry):
        for step in range(STEPS):
            exchange(step, unit).wait_send()
        return carry

    def wave(k, carry):
        def inner(step, carry):
            chunk = k - step - step // 2

            @pl.when((chunk == 0) & (step > 0))
            def _():
                prepare(step)
                turn_inputs(step)

            on_chunk(chunk, lambda unit, units: task(step, unit, units))
            return carry

        lax.fori_loop(0, STEPS, inner, 0)

        @pl.when(k == CHUNKS + LAST_LAG - 2)
        def _():
            def turn_back(tap, carry):
                new_v[tap] = jnp.transpose(vel[tap])
                new_w[tap, :, :128] = jnp.transpose(w_out[tap, :128])
                return carry

            lax.fori_loop(0, TAPS, turn_back, 0, unroll=True)

        @pl.when(k == CHUNKS + LAST_LAG - 1)
        def _():
            lax.fori_loop(0, UNITS, drain, 0)

        on_chunk(k - LAST_LAG, finish)
        return carry

    lax.fori_loop(0, CHUNKS + LAST_LAG, wave, 0)

    def turn_rest(tap, carry):
        new_w[tap, :, 128:] = jnp.transpose(w_out[tap, 128:])
        return carry

    lax.fori_loop(0, TAPS, turn_rest, 0, unroll=True)


def store(new_w, new_v, w_hbm, v_hbm, sem):
    copies = (
        pltpu.make_async_copy(new_w, w_hbm.at[0, 0], sem.at[0]),
        pltpu.make_async_copy(new_v, v_hbm.at[0, 0], sem.at[1]),
    )
    for copy in copies:
        copy.start()
    for copy in copies:
        copy.wait()


def body(clean, noise, noise_level, weight, velocity):
    hbm = pl.BlockSpec(memory_space=pl.ANY)
    out = pltpu.VMEM((TAPS, C, C), F32)
    vmem = pl.BlockSpec(memory_space=pltpu.VMEM)
    new_w, new_v = pl.pallas_call(
        kernel,
        out_shape=(out, out),
        in_specs=[pl.BlockSpec(memory_space=pltpu.SMEM), hbm, hbm, hbm, hbm],
        out_specs=(vmem, vmem),
        scratch_shapes=[
            pltpu.VMEM((STEPS, BATCH, C, CELLS), BF16),
            pltpu.VMEM((STEPS, BATCH, C, CELLS), BF16),
            pltpu.VMEM((TAPS, C, C), F32),
            pltpu.VMEM((TAPS, C, C), F32),
            pltpu.VMEM((STEPS, C, BATCH * CELLS), BF16),
            pltpu.VMEM((STEPS, C, BATCH * CELLS), BF16),
            pltpu.VMEM((STEPS, BATCH * CELLS, C), BF16),
            pltpu.VMEM((STEPS + 1, UNITS, TAPS, ROWS, 128), F32),
            pltpu.VMEM((STEPS + 1, UNITS, TAPS, ROWS, 128), F32),
            pltpu.VMEM((TAPS, C, C), F32),
            pltpu.VMEM((TAPS, C, C), F32),
            pltpu.SemaphoreType.DMA((2, STEPS)),
            pltpu.SemaphoreType.DMA((2,)),
            pltpu.SemaphoreType.DMA((STEPS, UNITS)),
            pltpu.SemaphoreType.DMA((STEPS, UNITS)),
        ],
        compiler_params=pltpu.CompilerParams(
            collective_id=0, has_side_effects=True, vmem_limit_bytes=52 << 20
        ),
        name="train",
    )(jnp.swapaxes(noise_level, 2, 3), clean, noise, weight, velocity)
    shape = jax.ShapeDtypeStruct((1, 1, TAPS, C, C), F32)
    return pl.pallas_call(
        store,
        out_shape=(shape, shape),
        in_specs=[vmem, vmem],
        out_specs=(hbm, hbm),
        scratch_shapes=[pltpu.SemaphoreType.DMA((2,))],
        name="store",
    )(pltpu.with_memory_space_constraint(new_w, pltpu.VMEM), pltpu.with_memory_space_constraint(new_v, pltpu.VMEM))


def solution(mesh):
    in_specs = (
        P("rx", "ry", None, None, None, None),
        P("rx", "ry", None, None, None, None),
        P("rx", "ry", None, None),
        P("rx", "ry", None, None, None),
        P("rx", "ry", None, None, None),
    )
    out_specs = (P("rx", "ry", None, None, None), P("rx", "ry", None, None, None))
    return jax.shard_map(body, mesh=mesh, in_specs=in_specs, out_specs=out_specs, check_vma=False)
```
